32 devices in a mesh: col: 16 (over z, x, core), row: 2 (over y).
Axes of the slice: x: 2, y: 2, z: 4, core: 2. Of those that a mesh axis runs over, the one named last changes fastest.
Arguments:
- uniq_rows: bfloat16 [32, 128, 1536], P('row', 'col'), may hold values from -6 to 6
- row_ids: int32 [32, 128, 8], P('row', 'col'), may hold values from 0 to 255, as said below
- sample_idx: int32 [512, 128], P('row', 'col'), may hold values from 0 to 7, as said below
- fm_proj: bfloat16 [128, 8], replicated, may hold values from -0.5 to 0.5
- ln_gain: float32 [1024], replicated, may hold values from 0.5 to 1.5
- w_up: bfloat16 [1024, 2048], P(None, 'row'), may hold values from -0.1875 to 0.1875
- w_down: bfloat16 [2048, 1536], P('row'), may hold values from -0.125 to 0.125
- w_lc: bfloat16 [8, 128], replicated, may hold values from -0.5 to 0.5
- w_res: bfloat16 [16, 128], replicated, may hold values from -0.5 to 0.5
- out_gain: float32 [192], replicated, may hold values from 0.5 to 1.5
- cotangent: bfloat16 [512, 3072], P(('row', 'col')), may hold values from -6 to 6
- moment1: float32 [128, 256, 192], P('col', 'row'), may hold values from -1.5 to 1.5
- moment2: float32 [128, 256], P('col', 'row'), may hold values from 0.01 to 0.1
Outputs:
- layer_out: bfloat16 [512, 3072], P(('row', 'col'))
- new_moment1: float32 [128, 256, 192], P('col', 'row')
- new_moment2: float32 [128, 256], P('col', 'row')
- row_step: float32 [128, 256, 192], P('col', 'row')
The draws below stay inside these ranges and needn't reach their ends.
Inputs may be any that keep to these rules, and one draw needn't show every extreme that they name: `sample_idx`: for each block of 16 samples and each slot, every one of the 8 list entries is used by at least one sample of the block. `row_ids`: the 8 ids of one list are distinct. Row v of a slot is owned by index v // 128 of row. Of the 1024 list entries held by one device (the blocks of its index of row, the slots of its index of col), at most 640 name rows of one owner, and in every draw some owner is named exactly 640 times on each device.
All inputs are finite; a program needn't handle non-finite values.
Results may differ from the reference program's by a relative error of at most 0.005.
Values may be sent and summed in bfloat16 or wider, within the bound.
A program may use at most 64 MiB of HBM per device.

```python
import math
import jax
import jax.numpy as jnp
from jax import lax

SLOTS = 128
E = 192
RANK = 8
HID = 2048
NF = 8
NL = 8
S_DEV = 16
V_DEV = 128
UNIQ = 8
SLOTS_DEV = 8
FLAT = 1024
NOUT = 16
NBLK = 32
SAMPLES = 512
VOCAB = 256
CAP = 640
N_COL = 16
N_ROW = 2


def draw_sample_idx(key, part):
    first, second = jax.random.split(key)
    filler = jax.random.randint(first, (NBLK, SLOTS, S_DEV), 0, UNIQ)
    scores = jax.random.randint(second, (NBLK, SLOTS, S_DEV), 0, 1 << 20) * S_DEV + jnp.arange(S_DEV, dtype=jnp.int32)
    order = jnp.argsort(scores, axis=-1)
    ranks = jnp.argsort(order, axis=-1).astype(jnp.int32)
    chosen = jnp.where(ranks < UNIQ, ranks, filler)
    return jnp.transpose(chosen, (0, 2, 1)).reshape(SAMPLES, SLOTS)


def draw_row_ids(key, part):
    keys = jax.random.split(key, 4)
    entries = SLOTS * UNIQ
    rest = entries - CAP
    share = rest // (N_ROW - 1)
    extra = rest % (N_ROW - 1)
    relative_owner = jnp.arange(N_ROW, dtype=jnp.int32)
    counts = jnp.where(relative_owner == 0, CAP, share + (relative_owner - 1 < extra).astype(jnp.int32))
    bounds = jnp.cumsum(counts)
    position = jnp.arange(entries, dtype=jnp.int32)
    relative = jnp.sum((position[:, None] >= bounds[None, :]).astype(jnp.int32), 1)
    busiest = jax.random.randint(keys[0], (N_COL,), 0, N_ROW)
    ordered = (relative[None, :] + busiest[:, None]) % N_ROW
    scores = jax.random.randint(keys[1], (N_ROW, N_COL, entries), 0, 1 << 16) * entries + position
    shuffle = jnp.argsort(scores, axis=-1)
    owner = jnp.take_along_axis(jnp.broadcast_to(ordered[None], (N_ROW, N_COL, entries)), shuffle, axis=-1)
    owner = owner.reshape(N_ROW, N_COL, N_COL, SLOTS_DEV, UNIQ)
    owner = jnp.transpose(owner, (0, 2, 1, 3, 4)).reshape(NBLK, SLOTS, UNIQ)
    offset = jax.random.randint(keys[2], (NBLK, SLOTS, 1), 0, V_DEV)
    stride = 2 * jax.random.randint(keys[3], (NBLK, SLOTS, 1), 0, max(V_DEV // 2, 1)) + 1
    local = (offset + jnp.arange(UNIQ, dtype=jnp.int32) * stride) % V_DEV
    return (owner * V_DEV + local).astype(jnp.int32)


def levels(rng, extent, pieces, smallest, high):
    def one(dim, shards_of):
        draws = jax.random.uniform(jax.random.fold_in(jax.random.fold_in(rng, 6), dim), (shards_of,), jnp.float32, smallest / len(pieces), high / len(pieces))
        return jnp.repeat(jnp.exp(draws), extent[dim] // shards_of).reshape((-1,) + (1,) * (len(extent) - dim - 1))

    level = one(*pieces[0])
    for cut in pieces[1:]:
        level = level * one(*cut)
    return level


def gaussian(stream_key, dims, width, reach, cuts=(), held_as=jnp.bfloat16):
    level = levels(stream_key, dims, cuts, -0.22, 0.18) if cuts else 1.0
    drawn = jax.random.normal(stream_key, dims, jnp.float32) * width * level
    return jnp.minimum(jnp.maximum(drawn, -reach), reach).astype(held_as)


def setup_inputs(seed: int = 0) -> dict:
    key_list = jax.random.split(jax.random.key(seed), 14)
    return {
        "uniq_rows": gaussian(key_list[0], (NBLK, SLOTS, UNIQ * E), 1.0, 6.0, ((0, 2), (1, 16))),
        "row_ids": draw_row_ids(jax.random.fold_in(key_list[13], 71), 0),
        "sample_idx": draw_sample_idx(jax.random.fold_in(key_list[13], 71), 0),
        "fm_proj": gaussian(key_list[3], (SLOTS, RANK), SLOTS ** -0.5, 0.5),
        "ln_gain": jnp.clip(1.0 + 0.1 * jax.random.normal(key_list[4], (FLAT,), jnp.float32), 0.5, 1.5),
        "w_up": gaussian(key_list[5], (FLAT, HID), FLAT ** -0.5, 0.1875, ((1, 2),)),
        "w_down": gaussian(key_list[6], (HID, NF * E), HID ** -0.5, 0.125, ((0, 2),)),
        "w_lc": gaussian(key_list[7], (NL, SLOTS), SLOTS ** -0.5, 0.5),
        "w_res": gaussian(key_list[8], (NOUT, SLOTS), SLOTS ** -0.5, 0.5),
        "out_gain": jnp.clip(1.0 + 0.1 * jax.random.normal(key_list[9], (E,), jnp.float32), 0.5, 1.5),
        "cotangent": gaussian(key_list[10], (SAMPLES, NOUT * E), 1.0, 6.0, ((0, 32),)),
        "moment1": gaussian(key_list[11], (SLOTS, VOCAB, E), 0.1, 1.5, ((0, 16), (1, 2)), jnp.float32),
        "moment2": jnp.clip(jnp.exp(math.log(0.1) - 2.3025851 * jax.random.uniform(key_list[12], (SLOTS, VOCAB), jnp.float32) ** levels(key_list[12], (SLOTS, VOCAB), ((0, 16), (1, 2)), -0.2, 0.2)), 0.01, 0.1),
    }


HIGH = lax.Precision.HIGHEST

def layer_norm(values, gain):
    centered = values - lax.optimization_barrier(jnp.mean(values, -1, keepdims=True))
    inverse = lax.rsqrt(lax.optimization_barrier(jnp.mean(centered * centered, -1, keepdims=True)) + 1e-05)
    normed = centered * inverse
    return (normed * gain, normed, inverse)

def norm_back(grad_out, normed, inverse):
    first = lax.optimization_barrier(jnp.mean(grad_out, -1, keepdims=True))
    second = lax.optimization_barrier(jnp.mean(grad_out * normed, -1, keepdims=True))
    return (grad_out - first - normed * second) * inverse

def silu_grad(values):
    sigma = jax.nn.sigmoid(values)
    return sigma * (1.0 + values * (1.0 - sigma))

def block_step(embed, cotangent, fm_proj, ln_gain, w_up, w_down, w_lc, w_res, out_gain):
    count = embed.shape[0]
    embed32 = embed.astype(jnp.float32)
    proj32 = fm_proj.astype(jnp.float32)
    lc32 = w_lc.astype(jnp.float32)
    res32 = w_res.astype(jnp.float32)
    compress = jnp.einsum('ste,tk->sek', embed32, proj32, precision=HIGH).astype(jnp.bfloat16)
    comp32 = compress.astype(jnp.float32)
    gram = jnp.einsum('ste,sek->stk', embed32, comp32, precision=HIGH)
    flat = gram.reshape(count, FLAT)
    scaled, normed_in, inverse_in = layer_norm(flat, ln_gain)
    normal_in = scaled.astype(jnp.bfloat16)
    hidden_pre = jnp.dot(normal_in, w_up, preferred_element_type=jnp.float32)
    hidden = jax.nn.silu(hidden_pre).astype(jnp.bfloat16)
    fm_out = jnp.dot(hidden, w_down, preferred_element_type=jnp.float32)
    linear = jnp.einsum('lt,ste->sle', lc32, embed32, precision=HIGH)
    joined = jnp.concatenate([fm_out.reshape(count, NF, E), linear], 1)
    normed_out, normed_rows, inverse_rows = layer_norm(joined, out_gain)
    residual = jnp.einsum('ot,ste->soe', res32, embed32, precision=HIGH)
    result = (normed_out + residual).reshape(count, NOUT * E).astype(jnp.bfloat16)
    upstream = cotangent.astype(jnp.float32).reshape(count, NOUT, E)
    grad_joined = norm_back(upstream * out_gain, normed_rows, inverse_rows)
    grad_fm = grad_joined[:, :NF].reshape(count, NF * E).astype(jnp.bfloat16)
    grad_hidden = lax.dot_general(grad_fm, w_down, (((1,), (1,)), ((), ())), preferred_element_type=jnp.float32)
    grad_pre = (grad_hidden * silu_grad(hidden_pre)).astype(jnp.bfloat16)
    grad_flat = lax.dot_general(grad_pre, w_up, (((1,), (1,)), ((), ())), preferred_element_type=jnp.float32)
    grad_gram = norm_back(grad_flat * ln_gain, normed_in, inverse_in).reshape(count, SLOTS, RANK)
    grad_embed = jnp.einsum('stk,sek->ste', grad_gram, comp32, precision=HIGH)
    grad_comp = jnp.einsum('ste,stk->sek', embed32, grad_gram, precision=HIGH)
    grad_embed = grad_embed + jnp.einsum('tk,sek->ste', proj32, grad_comp, precision=HIGH)
    grad_embed = grad_embed + jnp.einsum('lt,sle->ste', lc32, grad_joined[:, NF:], precision=HIGH)
    grad_embed = grad_embed + jnp.einsum('ot,soe->ste', res32, upstream, precision=HIGH)
    return (result, grad_embed)

def reference(uniq_rows, row_ids, sample_idx, fm_proj, ln_gain, w_up, w_down, w_lc, w_res, out_gain, cotangent, moment1, moment2):
    rows = uniq_rows.reshape(NBLK, SLOTS, UNIQ, E)
    index = sample_idx.reshape(NBLK, S_DEV, SLOTS)
    upstream = cotangent.reshape(NBLK, S_DEV, NOUT * E)
    slot_row = jnp.arange(SLOTS, dtype=jnp.int32)[None, :]
    slot_col = jnp.arange(SLOTS, dtype=jnp.int32)[:, None]

    def visit(grads, inputs):
        block_rows, block_index, block_cot, block_ids = inputs
        embed = block_rows[slot_row, block_index]
        result, grad_embed = block_step(embed, block_cot, fm_proj, ln_gain, w_up, w_down, w_lc, w_res, out_gain)
        list_grads = jnp.zeros((SLOTS, UNIQ, E), jnp.float32).at[jnp.broadcast_to(slot_row, block_index.shape), block_index].add(grad_embed)
        grads = grads.at[jnp.broadcast_to(slot_col, block_ids.shape), block_ids].add(list_grads)
        return (grads, result)
    start = jnp.zeros((SLOTS, VOCAB, E), jnp.float32)
    row_grads, outputs = lax.scan(visit, start, (rows, index, upstream, row_ids))
    layer_out = outputs.reshape(SAMPLES, NOUT * E)
    new_moment1 = 0.9 * moment1 + 0.1 * row_grads
    new_moment2 = 0.99 * moment2 + 0.01 * lax.optimization_barrier(jnp.mean(row_grads * row_grads, -1))
    row_step = new_moment1 * lax.rsqrt(new_moment2)[..., None]
    return (layer_out, new_moment1, new_moment2, row_step)
```

```python
import functools

import jax
import jax.numpy as jnp
from jax import lax
from jax.experimental import pallas as pl
from jax.experimental.pallas import tpu as pltpu
from jax.sharding import PartitionSpec as P

HIGH = lax.Precision.HIGHEST


def layer_norm(values, gain):
    centered = values - jnp.mean(values, -1, keepdims=True)
    inverse = lax.rsqrt(jnp.mean(centered * centered, -1, keepdims=True) + 1e-05)
    normed = centered * inverse
    return (normed * gain, normed, inverse)


def norm_back(grad_out, normed, inverse):
    first = jnp.mean(grad_out, -1, keepdims=True)
    second = jnp.mean(grad_out * normed, -1, keepdims=True)
    return (grad_out - first - normed * second) * inverse


def silu_grad(values):
    sigma = jax.nn.sigmoid(values)
    return sigma * (1.0 + values * (1.0 - sigma))


def plain_body(
    uniq_rows,
    row_ids,
    sample_idx,
    fm_proj,
    ln_gain,
    w_up,
    w_down,
    w_lc,
    w_res,
    out_gain,
    cotangent,
    moment1,
    moment2,
):
    columns = lax.axis_size("col")
    owners = lax.axis_size("row")
    slot_dev = uniq_rows.shape[1]
    width = out_gain.shape[0]
    uniq = uniq_rows.shape[2] // width
    samples = cotangent.shape[0]
    slots = slot_dev * columns
    vocab_dev = moment2.shape[1]
    rank = fm_proj.shape[1]
    fm_rows = w_down.shape[1] // width
    out_rows = w_res.shape[0]
    entry_iota = jnp.arange(uniq, dtype=jnp.int32)
    index_local = sample_idx.reshape(columns, samples, slot_dev)
    index = lax.all_to_all(index_local, "col", split_axis=0, concat_axis=2, tiled=True).reshape(
        samples, slots
    )
    picker = (index[:, :, None] == entry_iota).astype(jnp.bfloat16)
    moved = lax.all_to_all(uniq_rows, "col", split_axis=0, concat_axis=1, tiled=True)
    table = moved.reshape(slots, uniq, width)
    embed = jnp.einsum("stl,tle->ste", picker, table, preferred_element_type=jnp.float32).astype(
        jnp.bfloat16
    )
    compress = jnp.einsum("ste,tk->sek", embed, fm_proj, preferred_element_type=jnp.float32).astype(
        jnp.bfloat16
    )
    gram = jnp.einsum("ste,sek->stk", embed, compress, preferred_element_type=jnp.float32)
    flat = gram.reshape(samples, slots * rank)
    scaled, normed_in, inverse_in = layer_norm(flat, ln_gain)
    normal_in = scaled.astype(jnp.bfloat16)
    hidden_pre = jnp.dot(
        lax.all_gather(normal_in, "row", axis=0, tiled=True),
        w_up,
        preferred_element_type=jnp.float32,
    )
    hidden = jax.nn.silu(hidden_pre).astype(jnp.bfloat16)
    part_rows = hidden
    fm_out = lax.psum_scatter(
        jnp.dot(part_rows, w_down, preferred_element_type=jnp.float32),
        "row",
        scatter_dimension=0,
        tiled=True,
    )
    linear = jnp.einsum("lt,ste->sle", w_lc, embed, preferred_element_type=jnp.float32)
    joined = jnp.concatenate([fm_out.reshape(samples, fm_rows, width), linear], 1)
    normed_out, normed_rows, inverse_rows = layer_norm(joined, out_gain)
    residual = jnp.einsum("ot,ste->soe", w_res, embed, preferred_element_type=jnp.float32)
    layer_out = (normed_out + residual).reshape(samples, out_rows * width).astype(jnp.bfloat16)
    upstream = cotangent.astype(jnp.float32).reshape(samples, out_rows, width)
    grad_joined = norm_back(upstream * out_gain, normed_rows, inverse_rows)
    grad_fm = grad_joined[:, :fm_rows].reshape(samples, fm_rows * width).astype(jnp.bfloat16)
    grad_hidden = lax.dot_general(
        lax.all_gather(grad_fm, "row", axis=0, tiled=True),
        w_down,
        (((1,), (1,)), ((), ())),
        preferred_element_type=jnp.float32,
    )
    grad_pre = (grad_hidden * silu_grad(hidden_pre)).astype(jnp.bfloat16)
    part_rows = grad_pre
    grad_flat = lax.psum_scatter(
        lax.dot_general(
            part_rows, w_up, (((1,), (1,)), ((), ())), preferred_element_type=jnp.float32
        ).astype(jnp.bfloat16),
        "row",
        scatter_dimension=0,
        tiled=True,
    ).astype(jnp.float32)
    grad_gram = norm_back(grad_flat * ln_gain, normed_in, inverse_in).reshape(samples, slots, rank)
    grad_embed = jnp.einsum("stk,sek->ste", grad_gram, compress.astype(jnp.float32), precision=HIGH)
    grad_comp = jnp.einsum(
        "ste,stk->sek", embed, grad_gram, precision=HIGH, preferred_element_type=jnp.float32
    )
    grad_embed = grad_embed + jnp.einsum(
        "tk,sek->ste", fm_proj.astype(jnp.float32), grad_comp, precision=HIGH
    )
    grad_embed = grad_embed + jnp.einsum(
        "lt,sle->ste", w_lc.astype(jnp.float32), grad_joined[:, fm_rows:], precision=HIGH
    )
    grad_embed = grad_embed + jnp.einsum(
        "ot,soe->ste", w_res.astype(jnp.float32), upstream, precision=HIGH
    )
    list_grads = jnp.einsum("stl,ste->tle", picker.astype(jnp.float32), grad_embed, precision=HIGH)
    returned = lax.all_to_all(
        list_grads.reshape(columns, slot_dev, uniq * width),
        "col",
        split_axis=0,
        concat_axis=0,
        tiled=True,
    )
    entry_grads = returned.reshape(columns * slot_dev * uniq, width)
    row_list = row_ids.reshape(-1)
    slot_of = jnp.broadcast_to(
        jnp.arange(slot_dev, dtype=jnp.int32)[None, :, None], row_ids.shape
    ).reshape(-1)
    owner = row_list // vocab_dev
    target = slot_of * vocab_dev + row_list % vocab_dev
    span = slot_dev * vocab_dev
    entries = row_list.shape[0]
    capacity = 5 * entries // (4 * owners)
    onehot = (owner[:, None] == jnp.arange(owners, dtype=jnp.int32)).astype(jnp.int32)
    before = jnp.cumsum(onehot, 0) - onehot
    place = jnp.sum(before * onehot, 1)
    target_slot = owner * capacity + place
    bucket = jnp.zeros((owners * capacity, width), jnp.float32).at[target_slot].set(entry_grads)
    labels = (
        jnp.full((owners * capacity,), -1.0, jnp.float32)
        .at[target_slot]
        .set(target.astype(jnp.float32))
    )
    got_rows, got_labels = (
        lax.all_to_all(
            bucket.reshape(owners, capacity, width), "row", split_axis=0, concat_axis=0, tiled=True
        ),
        lax.all_to_all(
            labels.reshape(owners, capacity), "row", split_axis=0, concat_axis=0, tiled=True
        ),
    )
    segment = jnp.where(got_labels >= 0.0, got_labels, float(span)).astype(jnp.int32).reshape(-1)
    summed = jax.ops.segment_sum(got_rows.reshape(-1, width), segment, num_segments=span + 1)[:span]
    row_grads = summed.reshape(slot_dev, vocab_dev, width)
    new_moment1 = 0.9 * moment1 + 0.1 * row_grads
    new_moment2 = 0.99 * moment2 + 0.01 * jnp.mean(row_grads * row_grads, -1)
    row_step = new_moment1 * lax.rsqrt(new_moment2)[..., None]
    return (layer_out, new_moment1, new_moment2, row_step)


F32 = jnp.float32
BF16 = jnp.bfloat16
NT = (((1,), (1,)), ((), ()))


def iota(shape, dim):
    return lax.broadcasted_iota(jnp.int32, shape, dim)


def matmul(a, b, dims=(((1,), (0,)), ((), ())), precision=None):
    return lax.dot_general(a, b, dims, precision=precision, preferred_element_type=F32)


def fused_kernel(
    C,
    R,
    D,
    uniq,
    rid,
    sidx,
    fmp,
    gain,
    wup,
    wdn,
    wlc,
    wres,
    og,
    cot,
    lay_out,
    rg_out,
    land,
    iland,
    wraw,
    wp,
    wd,
    t32,
    tst,
    lm,
    lmask,
    arep,
    rmat,
    nrm,
    ggr,
    nall,
    y,
    ds,
    fown,
    fsend,
    frecv,
    fm,
    gall,
    qown,
    qsend,
    qrecv,
    lay32,
    gf32,
    lg,
    sb,
    rland,
    oh,
    enta,
    entb,
    owna,
    psa,
    pra,
    psb,
    prb,
    loc,
    s1,
    r1,
    si,
    ri,
    sa,
    ra,
    sbs,
    rbs,
    sx,
    rx,
):
    S, E, U, K, T = 16, 192, 8, 8, 128
    DV = D * T
    me = lax.axis_index("col")
    mr = lax.axis_index("row")

    def to_col(i):
        return lax.rem(me + i, C)

    def from_col(i):
        return lax.rem(me + C - i, C)

    def to_row(i):
        return lax.rem(mr + i, R)

    def from_row(i):
        return lax.rem(mr + R - i, R)

    def rcopy(src, dst, ssem, rsem, where):
        return pltpu.make_async_remote_copy(
            src_ref=src,
            dst_ref=dst,
            send_sem=ssem,
            recv_sem=rsem,
            device_id=where,
            device_id_type=pl.DeviceIdType.MESH,
        )

    cp_up = pltpu.make_async_copy(wup, wraw, loc.at[0])
    cp_dn = pltpu.make_async_copy(wdn, wd, loc.at[1])
    own_rows = pltpu.make_async_copy(uniq.at[me], land.at[me], loc.at[2])
    own_idx = pltpu.make_async_copy(sidx.at[me], iland.at[me], loc.at[3])
    cp_up.start()
    cp_dn.start()
    own_rows.start()
    own_idx.start()

    barrier = pltpu.get_barrier_semaphore()
    for i in range(1, C):
        pl.semaphore_signal(
            barrier, inc=1, device_id={"col": to_col(i)}, device_id_type=pl.DeviceIdType.MESH
        )
    for i in range(1, R):
        pl.semaphore_signal(
            barrier, inc=1, device_id={"row": to_row(i)}, device_id_type=pl.DeviceIdType.MESH
        )
    pl.semaphore_wait(barrier, C + R - 2)

    order = sorted(range(1, C), key=lambda i: -min(i, C - i))
    idx_copies, row_copies = [], []
    for i in order:
        p = to_col(i)
        idx_copies.append(rcopy(sidx.at[p], iland.at[me], si.at[i], ri.at[i], {"col": p}))
        idx_copies[-1].start()
    for i in order:
        p = to_col(i)
        row_copies.append(rcopy(uniq.at[p], land.at[me], s1.at[i], r1.at[i], {"col": p}))
        row_copies[-1].start()

    eye8 = (iota((K, K), 0) == iota((K, K), 1)).astype(F32)
    pr, pc = iota((256, 256), 0), iota((256, 256), 1)
    perm = (((pr & 31) * 8 + (pr >> 5)) == pc).astype(F32).astype(BF16)
    cp_up.wait()
    for g in range(4):
        blk = matmul(perm, wraw[g * 256 : (g + 1) * 256, :]).astype(BF16)
        for k in range(K):
            wp[k * T + g * 32 : k * T + (g + 1) * 32, :] = blk[k * 32 : (k + 1) * 32, :]
    lane = iota((K, K * T), 1)
    spread = jnp.where((lane & 7) == iota((K, K * T), 0), gain[...], 0.0)
    fold = ((iota((K * T, T), 0) >> 3) == iota((K * T, T), 1)).astype(F32)
    gk = matmul(spread, fold, precision=HIGH)

    amat = jnp.concatenate(
        [
            matmul(eye8.astype(BF16), fmp[...], NT),
            wlc[...].astype(F32),
            wres[...].astype(F32),
        ],
        0,
    )
    for j in range(32):
        arep[j * S : (j + 1) * S, :] = jnp.broadcast_to(amat[j : j + 1, :], (S, T))

    labels = matmul(eye8, rid[...].astype(F32).reshape(C * D, U), NT, HIGH).astype(jnp.int32)
    slot_lane = iota((U, T), 1) & (D - 1)
    target = iota((DV, T), 0)
    for i in range(R):
        local = labels - to_row(i) * T
        key = jnp.where((local >= 0) & (local < T), slot_lane * T + local, -1)
        for u in range(U):
            oh[i, :, u * T : (u + 1) * T] = jnp.where(
                target == jnp.broadcast_to(key[u : u + 1, :], (DV, T)), 1.0, 0.0
            ).astype(BF16)

    own_idx.wait()
    for cp in idx_copies:
        cp.wait_recv()
    ix = iland[...].astype(F32).reshape(C * S, D)
    tl = iota((C * S, T), 1)
    placed = jnp.zeros((C * S, T), F32)
    for d in range(D):
        placed = jnp.where((tl & (D - 1)) == d, ix[:, d : d + 1], placed)
    placed = jnp.where((tl >> (D.bit_length() - 1)) == (iota((C * S, T), 0) >> 4), placed, 0.0)
    ist = jnp.sum(placed.reshape(C, S, T), 0)
    idx_t = jnp.concatenate([ist] * 8, 0)
    idx_n = idx_t.T
    for u in range(U):
        for q in range(4):
            lm[q * T : (q + 1) * T, u * T : (u + 1) * T] = jnp.where(
                idx_t == float(u), arep[q * T : (q + 1) * T, :], 0.0
            ).astype(BF16)
    for q in range(4):
        turned = arep[q * T : (q + 1) * T, :].T
        for u in range(U):
            lmask[u * T : (u + 1) * T, q * T : (q + 1) * T] = jnp.where(
                idx_n == float(u), turned, 0.0
            ).astype(BF16)
    upstream = cot[...].astype(F32)
    for o in range(16):
        rmat[(16 + o) * S : (17 + o) * S, :] = upstream[:, o * E : (o + 1) * E].astype(BF16)

    own_rows.wait()
    for cp in row_copies:
        cp.wait_recv()
    t32[...] = land[...].astype(F32).reshape(T, U * E)
    for u in range(U):
        tst[u * T : (u + 1) * T, :] = t32[:, u * E : (u + 1) * E].astype(BF16)

    comp = matmul(lm[0:T, :], tst[...]).astype(BF16)
    rmat[512:640, :] = comp
    z = matmul(comp, tst[...], NT)
    gram = jnp.where(idx_t == 0.0, z[:, 0:T], 0.0)
    for u in range(1, U):
        gram = gram + jnp.where(idx_t == float(u), z[:, u * T : (u + 1) * T], 0.0)
    n_flat = float(K * T)
    g3 = gram.reshape(K, S, T)
    mu = jnp.sum(jnp.sum(g3, 0), -1, keepdims=True) / n_flat
    cent = g3 - mu[None]
    inv_in = lax.rsqrt(jnp.sum(jnp.sum(cent * cent, 0), -1, keepdims=True) / n_flat + 1e-05)
    normed_in = cent * inv_in[None]
    nrm[...] = normed_in.reshape(K * S, T)
    for k in range(K):
        nall[mr, :, k * T : (k + 1) * T] = (normed_in[k] * gk[k : k + 1, :]).astype(BF16)

    def row_send(stage, src_of, dst):
        copies = []
        for i in range(1, R):
            p = to_row(i)
            sem = stage * R + i
            copies.append(rcopy(src_of(p), dst.at[mr], sx.at[sem], rx.at[sem], {"row": p}))
            copies[-1].start()
        return copies

    n_copies = row_send(0, lambda p: nall.at[mr], nall)
    y[...] = matmul(lm[T:512, :], tst[...])
    cp_dn.wait()
    for cp in n_copies:
        cp.wait_recv()
    hp = matmul(nall[...].reshape(R * S, K * T), wp[...])
    sg = jax.nn.sigmoid(hp)
    hid = (hp * sg).astype(BF16)
    fp = matmul(hid, wd[...]).reshape(R, S, 8 * E)
    fsend[...] = fp.astype(BF16)
    fown[...] = fp
    f_copies = row_send(1, lambda p: fsend.at[p], frecv)
    ds[...] = sg * (1.0 + hp * (1.0 - sg))

    gain_out = og[...]

    def out_norm(joined, o):
        up = upstream[:, o * E : (o + 1) * E]
        c = joined - jnp.mean(joined, -1, keepdims=True)
        inv = lax.rsqrt(jnp.mean(c * c, -1, keepdims=True) + 1e-05)
        nr = c * inv
        return nr, norm_back(up * gain_out, nr, inv)

    for o in range(8, 16):
        nr, gj = out_norm(y[(o - 8) * S : (o - 7) * S, :], o)
        lay32[:, o * E : (o + 1) * E] = nr * gain_out + y[(8 + o) * S : (9 + o) * S, :]
        rmat[o * S : (o + 1) * S, :] = gj.astype(BF16)

    for cp in f_copies:
        cp.wait_recv()
    total = fown[mr]
    for i in range(1, R):
        total = total + frecv[from_row(i)].astype(F32)
    fm[...] = total
    for o in range(8):
        nr, gj = out_norm(fm[:, o * E : (o + 1) * E], o)
        lay32[:, o * E : (o + 1) * E] = nr * gain_out + y[(8 + o) * S : (9 + o) * S, :]
        gf32[:, o * E : (o + 1) * E] = gj
    gall[mr] = gf32[...].astype(BF16)
    g_copies = row_send(2, lambda p: gall.at[mr], gall)
    lay_out[...] = lay32[...].astype(BF16)
    for cp in g_copies:
        cp.wait_recv()
    gh = matmul(gall[...].reshape(R * S, 8 * E), wd[...], NT)
    gp = (gh * ds[...]).astype(BF16)
    gq = matmul(gp, wp[...], NT).reshape(R, S, K * T)
    qsend[...] = gq.astype(BF16)
    qown[...] = gq
    q_copies = row_send(3, lambda p: qsend.at[p], qrecv)
    for cp in q_copies:
        cp.wait_recv()
    gflat = qown[mr]
    for i in range(1, R):
        gflat = gflat + qrecv[from_row(i)].astype(F32)
    qs = [gflat[:, k * T : (k + 1) * T] * gk[k : k + 1, :] for k in range(K)]
    ns = [nrm[k * S : (k + 1) * S, :] for k in range(K)]
    first = jnp.sum(sum(qs), -1, keepdims=True) / n_flat
    second = jnp.sum(sum(q * n for q, n in zip(qs, ns)), -1, keepdims=True) / n_flat
    for k in range(K):
        ggr[k * S : (k + 1) * S, :] = (qs[k] - first - ns[k] * second) * inv_in
    gg = ggr[...]
    ggt = gg.T
    for u in range(U):
        lm[0:T, u * T : (u + 1) * T] = jnp.where(idx_t == float(u), gg, 0.0).astype(BF16)
        lmask[u * T : (u + 1) * T, 512:640] = jnp.where(idx_n == float(u), ggt, 0.0).astype(BF16)
    rmat[0:T, :] = matmul(lm[0:T, :], tst[...]).astype(BF16)
    lg[...] = matmul(lmask[...], rmat[...])

    half = iota((T, T), 1) < 64

    def lo(u):
        return lg[u * T : (u + 1) * T, 0:T].reshape(C, D, T)

    def hi(u):
        a = lg[u * T : (u + 1) * T, T:E]
        b = lg[(u + 4) * T : (u + 5) * T, T:E]
        return jnp.concatenate([a, b], 1).reshape(C, D, T)

    for p in range(2):
        sb[:, 64 + p * 16 : 80 + p * 16, :] = jnp.concatenate([hi(2 * p), hi(2 * p + 1)], 1).astype(
            BF16
        )
    for p in range(4):
        sb[:, p * 16 : (p + 1) * 16, :] = jnp.concatenate([lo(2 * p), lo(2 * p + 1)], 1).astype(
            BF16
        )
    cut_a, cut_b = pl.ds(0, 64), pl.ds(64, 32)
    b_copies, a_copies = [], []
    for i in order:
        p = to_col(i)
        b_copies.append(
            rcopy(sb.at[p, cut_b], rland.at[me, cut_b], sbs.at[i], rbs.at[i], {"col": p})
        )
        b_copies[-1].start()
    for i in order:
        p = to_col(i)
        a_copies.append(rcopy(sb.at[p, cut_a], rland.at[me, cut_a], sa.at[i], ra.at[i], {"col": p}))
        a_copies[-1].start()
    rland[me] = sb[me]

    for cp in b_copies:
        cp.wait_recv()
    for p in range(2):
        both = rland[:, 64 + p * 16 : 80 + p * 16, :].astype(F32)
        for h in range(2):
            u = 2 * p + h
            x = both[:, h * D : (h + 1) * D, :].reshape(T, T)
            entb[u * T : (u + 1) * T, :] = x.astype(BF16)
            entb[(u + 4) * T : (u + 5) * T, :] = pltpu.roll(x, 64, 1).astype(BF16)
    hd = DV // 2
    low = iota((hd, T), 1) < 64
    p_copies = []
    for i in range(1, R):
        full = matmul(oh[i], entb[...])
        psb[i] = jnp.where(low, full[:hd], pltpu.roll(full[hd:], 64, 1)).astype(BF16)
        p_copies.append(
            rcopy(psb.at[i], prb.at[i], sx.at[4 * R + i], rx.at[4 * R + i], {"row": to_row(i)})
        )
        p_copies[-1].start()
    rg_out[:, T:E] = matmul(oh[0], entb[...])[:, : E - T]

    for cp in a_copies:
        cp.wait_recv()
    for p in range(4):
        both = rland[:, p * 16 : (p + 1) * 16, :].astype(F32)
        for h in range(2):
            u = 2 * p + h
            enta[u * T : (u + 1) * T, :] = both[:, h * D : (h + 1) * D, :].reshape(T, T).astype(BF16)
    for i in range(1, R):
        psa[i] = matmul(oh[i], enta[...]).astype(BF16)
        p_copies.append(
            rcopy(psa.at[i], pra.at[i], sx.at[5 * R + i], rx.at[5 * R + i], {"row": to_row(i)})
        )
        p_copies[-1].start()
    owna[...] = matmul(oh[0], enta[...])
    for cp in p_copies:
        cp.wait_recv()
    total = owna[...]
    for i in range(1, R):
        total = total + pra[i].astype(F32)
    rg_out[:, 0:T] = total
    for i in range(1, R):
        x = prb[i].astype(F32)
        rg_out[:hd, T:E] += x[:, : E - T]
        rg_out[hd:, T:E] += pltpu.roll(x, 64, 1)[:, : E - T]

    for group in (
        idx_copies,
        row_copies,
        n_copies,
        f_copies,
        g_copies,
        q_copies,
        b_copies,
        a_copies,
        p_copies,
    ):
        for cp in group:
            cp.wait_send()


def fast_body(
    C,
    R,
    uniq_rows,
    row_ids,
    sample_idx,
    fm_proj,
    ln_gain,
    w_up,
    w_down,
    w_lc,
    w_res,
    out_gain,
    cotangent,
    moment1,
    moment2,
):
    D = uniq_rows.shape[1]
    S = cotangent.shape[0]
    hid = w_up.shape[1]
    wide = w_down.shape[1]
    flat = w_up.shape[0]
    width = out_gain.shape[0]
    T = C * D
    DV = D * T
    vmem = pl.BlockSpec(memory_space=pltpu.VMEM)
    hbm = pl.BlockSpec(memory_space=pl.ANY)
    dma = pltpu.SemaphoreType.DMA
    layer_out, row_grads = pl.pallas_call(
        functools.partial(fused_kernel, C, R, D),
        out_shape=(
            jax.ShapeDtypeStruct((S, 16 * width), BF16),
            jax.ShapeDtypeStruct((DV, width), F32),
        ),
        in_specs=[hbm, vmem, hbm, vmem, vmem, hbm, hbm, vmem, vmem, vmem, vmem],
        out_specs=(vmem, vmem),
        scratch_shapes=[
            pltpu.VMEM((C, D, wide), BF16),
            pltpu.VMEM((C, S, D), jnp.int32),
            pltpu.VMEM((flat, hid), BF16),
            pltpu.VMEM((flat, hid), BF16),
            pltpu.VMEM((hid, wide), BF16),
            pltpu.VMEM((T, wide), F32),
            pltpu.VMEM((8 * T, width), BF16),
            pltpu.VMEM((512, 8 * T), BF16),
            pltpu.VMEM((8 * T, 640), BF16),
            pltpu.VMEM((512, T), F32),
            pltpu.VMEM((640, width), BF16),
            pltpu.VMEM((128, T), F32),
            pltpu.VMEM((128, T), F32),
            pltpu.VMEM((R, S, flat), BF16),
            pltpu.VMEM((384, width), F32),
            pltpu.VMEM((R * S, hid), F32),
            pltpu.VMEM((R, S, wide), F32),
            pltpu.VMEM((R, S, wide), BF16),
            pltpu.VMEM((R, S, wide), BF16),
            pltpu.VMEM((S, wide), F32),
            pltpu.VMEM((R, S, wide), BF16),
            pltpu.VMEM((R, S, flat), F32),
            pltpu.VMEM((R, S, flat), BF16),
            pltpu.VMEM((R, S, flat), BF16),
            pltpu.VMEM((S, 16 * width), F32),
            pltpu.VMEM((S, wide), F32),
            pltpu.VMEM((8 * T, width), F32),
            pltpu.VMEM((C, 12 * D, T), BF16),
            pltpu.VMEM((C, 12 * D, T), BF16),
            pltpu.VMEM((R, DV, 8 * T), BF16),
            pltpu.VMEM((8 * T, T), BF16),
            pltpu.VMEM((8 * T, T), BF16),
            pltpu.VMEM((DV, T), F32),
            pltpu.VMEM((R, DV, T), BF16),
            pltpu.VMEM((R, DV, T), BF16),
            pltpu.VMEM((R, DV // 2, T), BF16),
            pltpu.VMEM((R, DV // 2, T), BF16),
            dma((4,)),
            dma((C,)),
            dma((C,)),
            dma((C,)),
            dma((C,)),
            dma((C,)),
            dma((C,)),
            dma((C,)),
            dma((C,)),
            dma((6 * R,)),
            dma((6 * R,)),
        ],
        compiler_params=pltpu.CompilerParams(
            collective_id=0, has_side_effects=True, vmem_limit_bytes=56 * 1024 * 1024
        ),
        name="wukong_step",
    )(
        uniq_rows,
        row_ids,
        sample_idx.reshape(C, S, D),
        fm_proj,
        ln_gain.reshape(1, flat),
        w_up,
        w_down,
        w_lc,
        w_res,
        out_gain.reshape(1, width),
        cotangent,
    )
    row_grads = row_grads.reshape(D, T, width)
    new_moment1 = 0.9 * moment1 + 0.1 * row_grads
    new_moment2 = 0.99 * moment2 + 0.01 * jnp.mean(row_grads * row_grads, -1)
    row_step = new_moment1 * lax.rsqrt(new_moment2)[..., None]
    return (layer_out, new_moment1, new_moment2, row_step)


def step(C, R, *args):
    if args[0].shape[1] == 8 and C == 16:
        return fast_body(C, R, *args)
    return plain_body(*args)


def solution(mesh):
    return jax.shard_map(
        functools.partial(step, mesh.shape["col"], mesh.shape["row"]),
        mesh=mesh,
        in_specs=(
            P("row", "col", None),
            P("row", "col", None),
            P("row", "col"),
            P(),
            P(),
            P(None, "row"),
            P("row", None),
            P(),
            P(),
            P(),
            P(("row", "col"), None),
            P("col", "row", None),
            P("col", "row"),
        ),
        out_specs=(
            P(("row", "col"), None),
            P("col", "row", None),
            P("col", "row"),
            P("col", "row", None),
        ),
        check_vma=False,
    )
```

```python
import functools

import jax
import jax.numpy as jnp
from jax import lax
from jax.experimental import pallas as pl
from jax.experimental.pallas import tpu as pltpu
from jax.sharding import PartitionSpec as P

HIGH = lax.Precision.HIGHEST


def layer_norm(values, gain):
    centered = values - jnp.mean(values, -1, keepdims=True)
    inverse = lax.rsqrt(jnp.mean(centered * centered, -1, keepdims=True) + 1e-05)
    normed = centered * inverse
    return (normed * gain, normed, inverse)


def norm_back(grad_out, normed, inverse):
    first = jnp.mean(grad_out, -1, keepdims=True)
    second = jnp.mean(grad_out * normed, -1, keepdims=True)
    return (grad_out - first - normed * second) * inverse


def silu_grad(values):
    sigma = jax.nn.sigmoid(values)
    return sigma * (1.0 + values * (1.0 - sigma))


def plain_body(
    uniq_rows,
    row_ids,
    sample_idx,
    fm_proj,
    ln_gain,
    w_up,
    w_down,
    w_lc,
    w_res,
    out_gain,
    cotangent,
    moment1,
    moment2,
):
    columns = lax.axis_size("col")
    owners = lax.axis_size("row")
    slot_dev = uniq_rows.shape[1]
    width = out_gain.shape[0]
    uniq = uniq_rows.shape[2] // width
    samples = cotangent.shape[0]
    slots = slot_dev * columns
    vocab_dev = moment2.shape[1]
    rank = fm_proj.shape[1]
    fm_rows = w_down.shape[1] // width
    out_rows = w_res.shape[0]
    entry_iota = jnp.arange(uniq, dtype=jnp.int32)
    index_local = sample_idx.reshape(columns, samples, slot_dev)
    index = lax.all_to_all(index_local, "col", split_axis=0, concat_axis=2, tiled=True).reshape(
        samples, slots
    )
    picker = (index[:, :, None] == entry_iota).astype(jnp.bfloat16)
    moved = lax.all_to_all(uniq_rows, "col", split_axis=0, concat_axis=1, tiled=True)
    table = moved.reshape(slots, uniq, width)
    embed = jnp.einsum("stl,tle->ste", picker, table, preferred_element_type=jnp.float32).astype(
        jnp.bfloat16
    )
    compress = jnp.einsum("ste,tk->sek", embed, fm_proj, preferred_element_type=jnp.float32).astype(
        jnp.bfloat16
    )
    gram = jnp.einsum("ste,sek->stk", embed, compress, preferred_element_type=jnp.float32)
    flat = gram.reshape(samples, slots * rank)
    scaled, normed_in, inverse_in = layer_norm(flat, ln_gain)
    normal_in = scaled.astype(jnp.bfloat16)
    hidden_pre = jnp.dot(
        lax.all_gather(normal_in, "row", axis=0, tiled=True),
        w_up,
        preferred_element_type=jnp.float32,
    )
    hidden = jax.nn.silu(hidden_pre).astype(jnp.bfloat16)
    part_rows = hidden
    fm_out = lax.psum_scatter(
        jnp.dot(part_rows, w_down, preferred_element_type=jnp.float32),
        "row",
        scatter_dimension=0,
        tiled=True,
    )
    linear = jnp.einsum("lt,ste->sle", w_lc, embed, preferred_element_type=jnp.float32)
    joined = jnp.concatenate([fm_out.reshape(samples, fm_rows, width), linear], 1)
    normed_out, normed_rows, inverse_rows = layer_norm(joined, out_gain)
    residual = jnp.einsum("ot,ste->soe", w_res, embed, preferred_element_type=jnp.float32)
    layer_out = (normed_out + residual).reshape(samples, out_rows * width).astype(jnp.bfloat16)
    upstream = cotangent.astype(jnp.float32).reshape(samples, out_rows, width)
    grad_joined = norm_back(upstream * out_gain, normed_rows, inverse_rows)
    grad_fm = grad_joined[:, :fm_rows].reshape(samples, fm_rows * width).astype(jnp.bfloat16)
    grad_hidden = lax.dot_general(
        lax.all_gather(grad_fm, "row", axis=0, tiled=True),
        w_down,
        (((1,), (1,)), ((), ())),
        preferred_element_type=jnp.float32,
    )
    grad_pre = (grad_hidden * silu_grad(hidden_pre)).astype(jnp.bfloat16)
    part_rows = grad_pre
    grad_flat = lax.psum_scatter(
        lax.dot_general(
            part_rows, w_up, (((1,), (1,)), ((), ())), preferred_element_type=jnp.float32
        ).astype(jnp.bfloat16),
        "row",
        scatter_dimension=0,
        tiled=True,
    ).astype(jnp.float32)
    grad_gram = norm_back(grad_flat * ln_gain, normed_in, inverse_in).reshape(samples, slots, rank)
    grad_embed = jnp.einsum("stk,sek->ste", grad_gram, compress.astype(jnp.float32), precision=HIGH)
    grad_comp = jnp.einsum(
        "ste,stk->sek", embed, grad_gram, precision=HIGH, preferred_element_type=jnp.float32
    )
    grad_embed = grad_embed + jnp.einsum(
        "tk,sek->ste", fm_proj.astype(jnp.float32), grad_comp, precision=HIGH
    )
    grad_embed = grad_embed + jnp.einsum(
        "lt,sle->ste", w_lc.astype(jnp.float32), grad_joined[:, fm_rows:], precision=HIGH
    )
    grad_embed = grad_embed + jnp.einsum(
        "ot,soe->ste", w_res.astype(jnp.float32), upstream, precision=HIGH
    )
    list_grads = jnp.einsum("stl,ste->tle", picker.astype(jnp.float32), grad_embed, precision=HIGH)
    returned = lax.all_to_all(
        list_grads.reshape(columns, slot_dev, uniq * width),
        "col",
        split_axis=0,
        concat_axis=0,
        tiled=True,
    )
    entry_grads = returned.reshape(columns * slot_dev * uniq, width)
    row_list = row_ids.reshape(-1)
    slot_of = jnp.broadcast_to(
        jnp.arange(slot_dev, dtype=jnp.int32)[None, :, None], row_ids.shape
    ).reshape(-1)
    owner = row_list // vocab_dev
    target = slot_of * vocab_dev + row_list % vocab_dev
    span = slot_dev * vocab_dev
    entries = row_list.shape[0]
    capacity = 5 * entries // (4 * owners)
    onehot = (owner[:, None] == jnp.arange(owners, dtype=jnp.int32)).astype(jnp.int32)
    before = jnp.cumsum(onehot, 0) - onehot
    place = jnp.sum(before * onehot, 1)
    target_slot = owner * capacity + place
    bucket = jnp.zeros((owners * capacity, width), jnp.float32).at[target_slot].set(entry_grads)
    labels = (
        jnp.full((owners * capacity,), -1.0, jnp.float32)
        .at[target_slot]
        .set(target.astype(jnp.float32))
    )
    got_rows, got_labels = (
        lax.all_to_all(
            bucket.reshape(owners, capacity, width), "row", split_axis=0, concat_axis=0, tiled=True
        ),
        lax.all_to_all(
            labels.reshape(owners, capacity), "row", split_axis=0, concat_axis=0, tiled=True
        ),
    )
    segment = jnp.where(got_labels >= 0.0, got_labels, float(span)).astype(jnp.int32).reshape(-1)
    summed = jax.ops.segment_sum(got_rows.reshape(-1, width), segment, num_segments=span + 1)[:span]
    row_grads = summed.reshape(slot_dev, vocab_dev, width)
    new_moment1 = 0.9 * moment1 + 0.1 * row_grads
    new_moment2 = 0.99 * moment2 + 0.01 * jnp.mean(row_grads * row_grads, -1)
    row_step = new_moment1 * lax.rsqrt(new_moment2)[..., None]
    return (layer_out, new_moment1, new_moment2, row_step)


F32 = jnp.float32
BF16 = jnp.bfloat16
NT = (((1,), (1,)), ((), ()))


def iota(shape, dim):
    return lax.broadcasted_iota(jnp.int32, shape, dim)


def matmul(a, b, dims=(((1,), (0,)), ((), ())), precision=None):
    return lax.dot_general(a, b, dims, precision=precision, preferred_element_type=F32)


def fused_kernel(
    C,
    R,
    D,
    uniq,
    rid,
    sidx,
    fmp,
    gain,
    wup,
    wdn,
    wlc,
    wres,
    og,
    cot,
    lay_out,
    rg_out,
    isend,
    land,
    iland,
    wraw,
    wp,
    wd,
    t32,
    tst,
    lm,
    lmask,
    arep,
    rmat,
    nrm,
    ggr,
    idxn,
    nall,
    y,
    ds,
    fown,
    fsend,
    frecv,
    fm,
    gall,
    qown,
    qsend,
    qrecv,
    lay32,
    gf32,
    lg,
    sb,
    rland,
    oh,
    ps,
    pr,
    loc,
    s1,
    r1,
    si,
    ri,
    sa,
    ra,
    sbs,
    rbs,
    sc,
    rc,
    sx,
    rx,
):
    S, E, U, K, T = 16, 192, 8, 8, 128
    me = lax.axis_index("col")
    mr = lax.axis_index("row")

    def to_col(i):
        return lax.rem(me + i, C)

    def from_col(i):
        return lax.rem(me + C - i, C)

    def to_row(i):
        return lax.rem(mr + i, R)

    def from_row(i):
        return lax.rem(mr + R - i, R)

    def rcopy(src, dst, ssem, rsem, where):
        return pltpu.make_async_remote_copy(
            src_ref=src,
            dst_ref=dst,
            send_sem=ssem,
            recv_sem=rsem,
            device_id=where,
            device_id_type=pl.DeviceIdType.MESH,
        )

    cp_up = pltpu.make_async_copy(wup, wraw, loc.at[0])
    cp_dn = pltpu.make_async_copy(wdn, wd, loc.at[1])
    own_rows = pltpu.make_async_copy(uniq.at[me], land.at[me], loc.at[2])
    cp_up.start()
    cp_dn.start()
    own_rows.start()

    barrier = pltpu.get_barrier_semaphore()
    for i in range(1, C):
        pl.semaphore_signal(
            barrier, inc=1, device_id={"col": to_col(i)}, device_id_type=pl.DeviceIdType.MESH
        )
    for i in range(1, R):
        pl.semaphore_signal(
            barrier, inc=1, device_id={"row": to_row(i)}, device_id_type=pl.DeviceIdType.MESH
        )
    for p in range(C):
        at = p * S % T
        tile = sidx[:, p * S // T * T : (p * S // T + 1) * T]
        if at:
            tile = pltpu.roll(tile, T - at, 1)
        isend[p] = tile[:, :S]
    iland[me] = isend[me]
    pl.semaphore_wait(barrier, C + R - 2)

    order = sorted(range(1, C), key=lambda i: -min(i, C - i))
    idx_copies, row_copies = [], []
    for i in order:
        p = to_col(i)
        idx_copies.append(rcopy(isend.at[p], iland.at[me], si.at[i], ri.at[i], {"col": p}))
        idx_copies[-1].start()
    for i in order:
        p = to_col(i)
        row_copies.append(rcopy(uniq.at[p], land.at[me], s1.at[i], r1.at[i], {"col": p}))
        row_copies[-1].start()

    to, at = iota((256, 256), 0), iota((256, 256), 1)
    perm = (((to & 31) * 8 + (to >> 5)) == at).astype(F32).astype(BF16)
    cp_up.wait()
    for g in range(4):
        blk = matmul(perm, wraw[g * 256 : (g + 1) * 256, :]).astype(BF16)
        for k in range(K):
            wp[k * T + g * 32 : k * T + (g + 1) * 32, :] = blk[k * 32 : (k + 1) * 32, :]
    lane = iota((K, K * T), 1)
    spread = jnp.where((lane & 7) == iota((K, K * T), 0), gain[...], 0.0)
    fold = ((iota((K * T, T), 0) >> 3) == iota((K * T, T), 1)).astype(F32)
    gk = matmul(spread, fold, precision=HIGH)

    amat = jnp.concatenate(
        [
            fmp[...].astype(F32),
            wlc[...].astype(F32),
            wres[...].astype(F32),
        ],
        0,
    )
    for j in range(32):
        arep[j * S : (j + 1) * S, :] = jnp.broadcast_to(amat[j : j + 1, :], (S, T))

    place = (iota((C, T), 0) == (iota((C, T), 1) >> 3)).astype(F32)
    wide = matmul(rid[...].astype(F32).reshape(D * U, C), place, precision=HIGH).reshape(D, U, T)
    mine = iota((D, U, T), 1) == (iota((D, U, T), 2) & (U - 1))
    labels = jnp.sum(jnp.where(mine, wide, 0.0), 1).astype(jnp.int32)
    target = iota((T, T), 0)
    for i in range(R):
        local = labels - to_row(i) * T
        for d in range(D):
            oh[i, d] = jnp.where(
                target == jnp.broadcast_to(local[d : d + 1, :], (T, T)), 1.0, 0.0
            ).astype(BF16)

    for cp in idx_copies:
        cp.wait_recv()
    ix = iland[...].astype(F32).reshape(T, S)
    tiled = (iota((S, T), 0) == (iota((S, T), 1) & (S - 1))).astype(F32)
    idx_n = matmul(ix, tiled, precision=HIGH)
    idxn[...] = idx_n
    idx_t = idx_n.T
    for u in range(U):
        for q in range(4):
            lm[q * T : (q + 1) * T, u * T : (u + 1) * T] = jnp.where(
                idx_t == float(u), arep[q * T : (q + 1) * T, :], 0.0
            ).astype(BF16)
    entry = iota((U, T), 0).astype(F32)

    def fill(src, q):
        for t in range(0, T, 2):
            rows = [
                jnp.where(
                    jnp.broadcast_to(idxn[v : v + 1, :], (U, T)) == entry,
                    jnp.broadcast_to(src[v : v + 1, :], (U, T)),
                    0.0,
                )
                for v in (t, t + 1)
            ]
            lmask[t * U : (t + 2) * U, q * T : (q + 1) * T] = jnp.concatenate(rows, 0).astype(BF16)

    for q in range(4):
        ggr[...] = arep[q * T : (q + 1) * T, :].T
        fill(ggr, q)
    upstream = cot[...].astype(F32)
    for o in range(16):
        rmat[(16 + o) * S : (17 + o) * S, :] = upstream[:, o * E : (o + 1) * E].astype(BF16)

    own_rows.wait()
    for cp in row_copies:
        cp.wait_recv()
    t32[...] = land[...].astype(F32).reshape(T, U * E)
    for u in range(U):
        tst[u * T : (u + 1) * T, :] = t32[:, u * E : (u + 1) * E].astype(BF16)

    comp = matmul(lm[0:T, :], tst[...]).astype(BF16)
    rmat[512:640, :] = comp
    z = matmul(comp, tst[...], NT)
    gram = jnp.where(idx_t == 0.0, z[:, 0:T], 0.0)
    for u in range(1, U):
        gram = gram + jnp.where(idx_t == float(u), z[:, u * T : (u + 1) * T], 0.0)
    n_flat = float(K * T)
    g3 = gram.reshape(K, S, T)
    mu = jnp.sum(jnp.sum(g3, 0), -1, keepdims=True) / n_flat
    cent = g3 - mu[None]
    inv_in = lax.rsqrt(jnp.sum(jnp.sum(cent * cent, 0), -1, keepdims=True) / n_flat + 1e-05)
    normed_in = cent * inv_in[None]
    nrm[...] = normed_in.reshape(K * S, T)
    for k in range(K):
        nall[mr, :, k * T : (k + 1) * T] = (normed_in[k] * gk[k : k + 1, :]).astype(BF16)

    def row_send(stage, src_of, dst):
        copies = []
        for i in range(1, R):
            p = to_row(i)
            sem = stage * R + i
            copies.append(rcopy(src_of(p), dst.at[mr], sx.at[sem], rx.at[sem], {"row": p}))
            copies[-1].start()
        return copies

    n_copies = row_send(0, lambda p: nall.at[mr], nall)
    y[...] = matmul(lm[T:512, :], tst[...])
    cp_dn.wait()
    for cp in n_copies:
        cp.wait_recv()
    hp = matmul(nall[...].reshape(R * S, K * T), wp[...])
    sg = jax.nn.sigmoid(hp)
    hid = (hp * sg).astype(BF16)
    fp = matmul(hid, wd[...]).reshape(R, S, 8 * E)
    fsend[...] = fp.astype(BF16)
    fown[...] = fp
    f_copies = row_send(1, lambda p: fsend.at[p], frecv)
    ds[...] = sg * (1.0 + hp * (1.0 - sg))

    gain_out = og[...]

    def out_norm(joined, o):
        up = upstream[:, o * E : (o + 1) * E]
        c = joined - jnp.mean(joined, -1, keepdims=True)
        inv = lax.rsqrt(jnp.mean(c * c, -1, keepdims=True) + 1e-05)
        nr = c * inv
        return nr, norm_back(up * gain_out, nr, inv)

    for o in range(8, 16):
        nr, gj = out_norm(y[(o - 8) * S : (o - 7) * S, :], o)
        lay32[:, o * E : (o + 1) * E] = nr * gain_out + y[(8 + o) * S : (9 + o) * S, :]
        rmat[o * S : (o + 1) * S, :] = gj.astype(BF16)

    for cp in f_copies:
        cp.wait_recv()
    total = fown[mr]
    for i in range(1, R):
        total = total + frecv[from_row(i)].astype(F32)
    fm[...] = total
    for o in range(8):
        nr, gj = out_norm(fm[:, o * E : (o + 1) * E], o)
        lay32[:, o * E : (o + 1) * E] = nr * gain_out + y[(8 + o) * S : (9 + o) * S, :]
        gf32[:, o * E : (o + 1) * E] = gj
    gall[mr] = gf32[...].astype(BF16)
    g_copies = row_send(2, lambda p: gall.at[mr], gall)
    lay_out[...] = lay32[...].astype(BF16)
    for cp in g_copies:
        cp.wait_recv()
    gh = matmul(gall[...].reshape(R * S, 8 * E), wd[...], NT)
    gp = (gh * ds[...]).astype(BF16)
    gq = matmul(gp, wp[...], NT).reshape(R, S, K * T)
    qsend[...] = gq.astype(BF16)
    qown[...] = gq
    q_copies = row_send(3, lambda p: qsend.at[p], qrecv)
    for cp in q_copies:
        cp.wait_recv()
    gflat = qown[mr]
    for i in range(1, R):
        gflat = gflat + qrecv[from_row(i)].astype(F32)
    qs = [gflat[:, k * T : (k + 1) * T] * gk[k : k + 1, :] for k in range(K)]
    ns = [nrm[k * S : (k + 1) * S, :] for k in range(K)]
    first = jnp.sum(sum(qs), -1, keepdims=True) / n_flat
    second = jnp.sum(sum(q * n for q, n in zip(qs, ns)), -1, keepdims=True) / n_flat
    for k in range(K):
        ggr[k * S : (k + 1) * S, :] = (qs[k] - first - ns[k] * second) * inv_in
    gg = ggr[...]
    for u in range(U):
        lm[0:T, u * T : (u + 1) * T] = jnp.where(idx_t == float(u), gg, 0.0).astype(BF16)
    ggr[...] = gg.T
    fill(ggr, 4)
    rmat[0:T, :] = matmul(lm[0:T, :], tst[...]).astype(BF16)
    lg[...] = matmul(lmask[...], rmat[...])

    top = lg[:, T:E].reshape(C, D * U, E - T)
    sb[:, 64:96, :] = jnp.concatenate([top[:, :32], top[:, 32:]], -1).astype(BF16)
    sb[:, 0:64, :] = lg[:, 0:T].reshape(C, D * U, T).astype(BF16)
    cuts = (pl.ds(64, 32), pl.ds(0, 32), pl.ds(32, 32))
    sems = ((sbs, rbs), (sa, ra), (sc, rc))
    g_in = []
    for cut, (ssem, rsem) in zip(cuts, sems):
        g_in.append([])
        for i in order:
            p = to_col(i)
            g_in[-1].append(
                rcopy(sb.at[p, cut], rland.at[me, cut], ssem.at[i], rsem.at[i], {"col": p})
            )
            g_in[-1][-1].start()
    rland[me] = sb[me]

    p_copies = []
    for stage in range(3):
        for cp in g_in[stage]:
            cp.wait_recv()
        pieces = []
        for p in range(2):
            start = (64, 0, 32)[stage] + p * 16
            both = rland[:, start : start + 16, :].astype(F32)
            for h in range(2):
                x = both[:, h * U : (h + 1) * U, :].reshape(T, T).T.astype(BF16)
                d = 2 * p + h
                if stage == 0:
                    pieces.append((d, T, E, x[: E - T]))
                    pieces.append((d + 4, T, E, x[E - T :]))
                else:
                    pieces.append((d + 4 * (stage - 1), 0, T, x))
        for i in range(1, R):
            for d, a, b, x in pieces:
                ps[i, d, a:b, :] = matmul(x, oh[i, d], NT).astype(BF16)
            part = (slice(0, D), slice(T, E)) if stage == 0 else (
                slice(4 * (stage - 1), 4 * stage),
                slice(0, T),
            )
            ds_of = tuple(pl.ds(q.start, q.stop - q.start) for q in part)
            sem = (4 + stage) * R + i
            p_copies.append(
                rcopy(
                    ps.at[(i,) + ds_of],
                    pr.at[(i,) + ds_of],
                    sx.at[sem],
                    rx.at[sem],
                    {"row": to_row(i)},
                )
            )
            p_copies[-1].start()
        for d, a, b, x in pieces:
            rg_out[d, a:b, :] = matmul(x, oh[0, d], NT)
    for cp in p_copies:
        cp.wait_recv()
    for i in range(1, R):
        rg_out[...] += pr[i].astype(F32)

    for group in (
        idx_copies,
        row_copies,
        n_copies,
        f_copies,
        g_copies,
        q_copies,
        g_in[0],
        g_in[1],
        g_in[2],
        p_copies,
    ):
        for cp in group:
            cp.wait_send()


def moment_kernel(width, lay, grads, m1, m2, lay_out, m1_out, m2_out, step_out):
    lay_out[...] = lay[...]
    for h in range(2):
        row = pl.ds(pl.program_id(0) * 2 + h, 1)
        g = grads[h]
        first = 0.9 * m1[h] + 0.1 * g
        second = 0.99 * m2[row, :] + 0.01 * (jnp.sum(g * g, 0, keepdims=True) / width)
        m1_out[h] = first
        m2_out[row, :] = second
        step_out[h] = first * lax.rsqrt(second)


def fast_body(
    C,
    R,
    uniq_rows,
    row_ids,
    sample_idx,
    fm_proj,
    ln_gain,
    w_up,
    w_down,
    w_lc,
    w_res,
    out_gain,
    cotangent,
    moment1,
    moment2,
):
    D = uniq_rows.shape[1]
    S = cotangent.shape[0]
    hid = w_up.shape[1]
    wide = w_down.shape[1]
    flat = w_up.shape[0]
    width = out_gain.shape[0]
    T = C * D
    vmem = pl.BlockSpec(memory_space=pltpu.VMEM)
    hbm = pl.BlockSpec(memory_space=pl.ANY)
    dma = pltpu.SemaphoreType.DMA
    layer_out, row_grads = pl.pallas_call(
        functools.partial(fused_kernel, C, R, D),
        out_shape=(
            jax.ShapeDtypeStruct((S, 16 * width), BF16),
            jax.ShapeDtypeStruct((D, width, T), F32),
        ),
        in_specs=[hbm, vmem, vmem, vmem, vmem, hbm, hbm, vmem, vmem, vmem, vmem],
        out_specs=(vmem, vmem),
        scratch_shapes=[
            pltpu.VMEM((C, D, S), jnp.int32),
            pltpu.VMEM((C, D, wide), BF16),
            pltpu.VMEM((C, D, S), jnp.int32),
            pltpu.VMEM((flat, hid), BF16),
            pltpu.VMEM((flat, hid), BF16),
            pltpu.VMEM((hid, wide), BF16),
            pltpu.VMEM((T, wide), F32),
            pltpu.VMEM((8 * T, width), BF16),
            pltpu.VMEM((512, 8 * T), BF16),
            pltpu.VMEM((8 * T, 640), BF16),
            pltpu.VMEM((512, T), F32),
            pltpu.VMEM((640, width), BF16),
            pltpu.VMEM((128, T), F32),
            pltpu.VMEM((128, T), F32),
            pltpu.VMEM((T, 128), F32),
            pltpu.VMEM((R, S, flat), BF16),
            pltpu.VMEM((384, width), F32),
            pltpu.VMEM((R * S, hid), F32),
            pltpu.VMEM((R, S, wide), F32),
            pltpu.VMEM((R, S, wide), BF16),
            pltpu.VMEM((R, S, wide), BF16),
            pltpu.VMEM((S, wide), F32),
            pltpu.VMEM((R, S, wide), BF16),
            pltpu.VMEM((R, S, flat), F32),
            pltpu.VMEM((R, S, flat), BF16),
            pltpu.VMEM((R, S, flat), BF16),
            pltpu.VMEM((S, 16 * width), F32),
            pltpu.VMEM((S, wide), F32),
            pltpu.VMEM((8 * T, width), F32),
            pltpu.VMEM((C, 12 * D, T), BF16),
            pltpu.VMEM((C, 12 * D, T), BF16),
            pltpu.VMEM((R, D, T, T), BF16),
            pltpu.VMEM((R, D, width, T), BF16),
            pltpu.VMEM((R, D, width, T), BF16),
            dma((4,)),
            dma((C,)),
            dma((C,)),
            dma((C,)),
            dma((C,)),
            dma((C,)),
            dma((C,)),
            dma((C,)),
            dma((C,)),
            dma((C,)),
            dma((C,)),
            dma((7 * R,)),
            dma((7 * R,)),
        ],
        compiler_params=pltpu.CompilerParams(
            collective_id=0, has_side_effects=True, vmem_limit_bytes=56 * 1024 * 1024
        ),
        name="wukong_step",
    )(
        uniq_rows,
        row_ids.transpose(1, 2, 0),
        sample_idx.T,
        fm_proj.T,
        ln_gain.reshape(1, flat),
        w_up,
        w_down,
        w_lc,
        w_res,
        out_gain.reshape(1, width),
        cotangent,
    )
    slab = pl.BlockSpec((2, width, T), lambda d: (d, 0, 0))
    whole = pl.BlockSpec((D, T), lambda d: (0, 0))
    strip = pl.BlockSpec((S, 8 * width // (D // 4)), lambda d: (0, d))
    layer_out, new_moment1, new_moment2, row_step = pl.pallas_call(
        functools.partial(moment_kernel, width),
        grid=(D // 2,),
        out_shape=(
            jax.ShapeDtypeStruct((S, 16 * width), BF16),
            jax.ShapeDtypeStruct((D, width, T), F32),
            jax.ShapeDtypeStruct((D, T), F32),
            jax.ShapeDtypeStruct((D, width, T), F32),
        ),
        in_specs=[strip, slab, slab, whole],
        out_specs=(strip, slab, whole, slab),
        name="moments",
    )(layer_out, row_grads, moment1.transpose(0, 2, 1), moment2)
    return (
        layer_out,
        new_moment1.transpose(0, 2, 1),
        new_moment2,
        row_step.transpose(0, 2, 1),
    )


def step(C, R, *args):
    if args[0].shape[1] == 8 and C == 16:
        return fast_body(C, R, *args)
    return plain_body(*args)


def solution(mesh):
    return jax.shard_map(
        functools.partial(step, mesh.shape["col"], mesh.shape["row"]),
        mesh=mesh,
        in_specs=(
            P("row", "col", None),
            P("row", "col", None),
            P("row", "col"),
            P(),
            P(),
            P(None, "row"),
            P("row", None),
            P(),
            P(),
            P(),
            P(("row", "col"), None),
            P("col", "row", None),
            P("col", "row"),
        ),
        out_specs=(
            P(("row", "col"), None),
            P("col", "row", None),
            P("col", "row"),
            P("col", "row", None),
        ),
        check_vma=False,
    )
```

```python
import functools

import jax
import jax.numpy as jnp
from jax import lax
from jax.experimental import pallas as pl
from jax.experimental.pallas import tpu as pltpu
from jax.sharding import PartitionSpec as P

HIGH = lax.Precision.HIGHEST


def layer_norm(values, gain):
    centered = values - jnp.mean(values, -1, keepdims=True)
    inverse = lax.rsqrt(jnp.mean(centered * centered, -1, keepdims=True) + 1e-05)
    normed = centered * inverse
    return (normed * gain, normed, inverse)


def norm_back(grad_out, normed, inverse):
    first = jnp.mean(grad_out, -1, keepdims=True)
    second = jnp.mean(grad_out * normed, -1, keepdims=True)
    return (grad_out - first - normed * second) * inverse


def silu_grad(values):
    sigma = jax.nn.sigmoid(values)
    return sigma * (1.0 + values * (1.0 - sigma))


def plain_body(
    uniq_rows,
    row_ids,
    sample_idx,
    fm_proj,
    ln_gain,
    w_up,
    w_down,
    w_lc,
    w_res,
    out_gain,
    cotangent,
    moment1,
    moment2,
):
    columns = lax.axis_size("col")
    owners = lax.axis_size("row")
    slot_dev = uniq_rows.shape[1]
    width = out_gain.shape[0]
    uniq = uniq_rows.shape[2] // width
    samples = cotangent.shape[0]
    slots = slot_dev * columns
    vocab_dev = moment2.shape[1]
    rank = fm_proj.shape[1]
    fm_rows = w_down.shape[1] // width
    out_rows = w_res.shape[0]
    entry_iota = jnp.arange(uniq, dtype=jnp.int32)
    index_local = sample_idx.reshape(columns, samples, slot_dev)
    index = lax.all_to_all(index_local, "col", split_axis=0, concat_axis=2, tiled=True).reshape(
        samples, slots
    )
    picker = (index[:, :, None] == entry_iota).astype(jnp.bfloat16)
    moved = lax.all_to_all(uniq_rows, "col", split_axis=0, concat_axis=1, tiled=True)
    table = moved.reshape(slots, uniq, width)
    embed = jnp.einsum("stl,tle->ste", picker, table, preferred_element_type=jnp.float32).astype(
        jnp.bfloat16
    )
    compress = jnp.einsum("ste,tk->sek", embed, fm_proj, preferred_element_type=jnp.float32).astype(
        jnp.bfloat16
    )
    gram = jnp.einsum("ste,sek->stk", embed, compress, preferred_element_type=jnp.float32)
    flat = gram.reshape(samples, slots * rank)
    scaled, normed_in, inverse_in = layer_norm(flat, ln_gain)
    normal_in = scaled.astype(jnp.bfloat16)
    hidden_pre = jnp.dot(
        lax.all_gather(normal_in, "row", axis=0, tiled=True),
        w_up,
        preferred_element_type=jnp.float32,
    )
    hidden = jax.nn.silu(hidden_pre).astype(jnp.bfloat16)
    part_rows = hidden
    fm_out = lax.psum_scatter(
        jnp.dot(part_rows, w_down, preferred_element_type=jnp.float32),
        "row",
        scatter_dimension=0,
        tiled=True,
    )
    linear = jnp.einsum("lt,ste->sle", w_lc, embed, preferred_element_type=jnp.float32)
    joined = jnp.concatenate([fm_out.reshape(samples, fm_rows, width), linear], 1)
    normed_out, normed_rows, inverse_rows = layer_norm(joined, out_gain)
    residual = jnp.einsum("ot,ste->soe", w_res, embed, preferred_element_type=jnp.float32)
    layer_out = (normed_out + residual).reshape(samples, out_rows * width).astype(jnp.bfloat16)
    upstream = cotangent.astype(jnp.float32).reshape(samples, out_rows, width)
    grad_joined = norm_back(upstream * out_gain, normed_rows, inverse_rows)
    grad_fm = grad_joined[:, :fm_rows].reshape(samples, fm_rows * width).astype(jnp.bfloat16)
    grad_hidden = lax.dot_general(
        lax.all_gather(grad_fm, "row", axis=0, tiled=True),
        w_down,
        (((1,), (1,)), ((), ())),
        preferred_element_type=jnp.float32,
    )
    grad_pre = (grad_hidden * silu_grad(hidden_pre)).astype(jnp.bfloat16)
    part_rows = grad_pre
    grad_flat = lax.psum_scatter(
        lax.dot_general(
            part_rows, w_up, (((1,), (1,)), ((), ())), preferred_element_type=jnp.float32
        ).astype(jnp.bfloat16),
        "row",
        scatter_dimension=0,
        tiled=True,
    ).astype(jnp.float32)
    grad_gram = norm_back(grad_flat * ln_gain, normed_in, inverse_in).reshape(samples, slots, rank)
    grad_embed = jnp.einsum("stk,sek->ste", grad_gram, compress.astype(jnp.float32), precision=HIGH)
    grad_comp = jnp.einsum(
        "ste,stk->sek", embed, grad_gram, precision=HIGH, preferred_element_type=jnp.float32
    )
    grad_embed = grad_embed + jnp.einsum(
        "tk,sek->ste", fm_proj.astype(jnp.float32), grad_comp, precision=HIGH
    )
    grad_embed = grad_embed + jnp.einsum(
        "lt,sle->ste", w_lc.astype(jnp.float32), grad_joined[:, fm_rows:], precision=HIGH
    )
    grad_embed = grad_embed + jnp.einsum(
        "ot,soe->ste", w_res.astype(jnp.float32), upstream, precision=HIGH
    )
    list_grads = jnp.einsum("stl,ste->tle", picker.astype(jnp.float32), grad_embed, precision=HIGH)
    returned = lax.all_to_all(
        list_grads.reshape(columns, slot_dev, uniq * width),
        "col",
        split_axis=0,
        concat_axis=0,
        tiled=True,
    )
    entry_grads = returned.reshape(columns * slot_dev * uniq, width)
    row_list = row_ids.reshape(-1)
    slot_of = jnp.broadcast_to(
        jnp.arange(slot_dev, dtype=jnp.int32)[None, :, None], row_ids.shape
    ).reshape(-1)
    owner = row_list // vocab_dev
    target = slot_of * vocab_dev + row_list % vocab_dev
    span = slot_dev * vocab_dev
    entries = row_list.shape[0]
    capacity = 5 * entries // (4 * owners)
    onehot = (owner[:, None] == jnp.arange(owners, dtype=jnp.int32)).astype(jnp.int32)
    before = jnp.cumsum(onehot, 0) - onehot
    place = jnp.sum(before * onehot, 1)
    target_slot = owner * capacity + place
    bucket = jnp.zeros((owners * capacity, width), jnp.float32).at[target_slot].set(entry_grads)
    labels = (
        jnp.full((owners * capacity,), -1.0, jnp.float32)
        .at[target_slot]
        .set(target.astype(jnp.float32))
    )
    got_rows, got_labels = (
        lax.all_to_all(
            bucket.reshape(owners, capacity, width), "row", split_axis=0, concat_axis=0, tiled=True
        ),
        lax.all_to_all(
            labels.reshape(owners, capacity), "row", split_axis=0, concat_axis=0, tiled=True
        ),
    )
    segment = jnp.where(got_labels >= 0.0, got_labels, float(span)).astype(jnp.int32).reshape(-1)
    summed = jax.ops.segment_sum(got_rows.reshape(-1, width), segment, num_segments=span + 1)[:span]
    row_grads = summed.reshape(slot_dev, vocab_dev, width)
    new_moment1 = 0.9 * moment1 + 0.1 * row_grads
    new_moment2 = 0.99 * moment2 + 0.01 * jnp.mean(row_grads * row_grads, -1)
    row_step = new_moment1 * lax.rsqrt(new_moment2)[..., None]
    return (layer_out, new_moment1, new_moment2, row_step)


F32 = jnp.float32
BF16 = jnp.bfloat16
NT = (((1,), (1,)), ((), ()))


def iota(shape, dim):
    return lax.broadcasted_iota(jnp.int32, shape, dim)


def matmul(a, b, dims=(((1,), (0,)), ((), ())), precision=None):
    return lax.dot_general(a, b, dims, precision=precision, preferred_element_type=F32)


def fused_kernel(
    C,
    R,
    D,
    uniq,
    rid,
    sidx,
    fmp,
    gain,
    wup,
    wdn,
    wlc,
    wres,
    og,
    cot,
    lay_out,
    rg_out,
    isend,
    land,
    iland,
    wraw,
    wp,
    wd,
    t32,
    tst,
    lm,
    lmask,
    arep,
    rmat,
    nrm,
    ggr,
    idxn,
    nall,
    y,
    ds,
    fown,
    fsend,
    frecv,
    fm,
    gall,
    qown,
    qsend,
    qrecv,
    lay32,
    gf32,
    lg,
    sb,
    rland,
    oh,
    ps,
    pr,
    loc,
    s1,
    r1,
    si,
    ri,
    sa,
    ra,
    sbs,
    rbs,
    sc,
    rc,
    sx,
    rx,
):
    S, E, U, K, T = 16, 192, 8, 8, 128
    me = lax.axis_index("col")
    mr = lax.axis_index("row")

    def to_col(i):
        return lax.rem(me + i, C)

    def from_col(i):
        return lax.rem(me + C - i, C)

    def to_row(i):
        return lax.rem(mr + i, R)

    def from_row(i):
        return lax.rem(mr + R - i, R)

    def rcopy(src, dst, ssem, rsem, where):
        return pltpu.make_async_remote_copy(
            src_ref=src,
            dst_ref=dst,
            send_sem=ssem,
            recv_sem=rsem,
            device_id=where,
            device_id_type=pl.DeviceIdType.MESH,
        )

    cp_up = pltpu.make_async_copy(wup, wraw, loc.at[0])
    cp_dn = pltpu.make_async_copy(wdn, wd, loc.at[1])
    own_rows = pltpu.make_async_copy(uniq.at[me], land.at[me], loc.at[2])
    own_rows.start()

    barrier = pltpu.get_barrier_semaphore()
    for i in range(1, C):
        pl.semaphore_signal(
            barrier, inc=1, device_id={"col": to_col(i)}, device_id_type=pl.DeviceIdType.MESH
        )
    for i in range(1, R):
        pl.semaphore_signal(
            barrier, inc=1, device_id={"row": to_row(i)}, device_id_type=pl.DeviceIdType.MESH
        )
    for p in range(C):
        at = p * S % T
        tile = sidx[:, p * S // T * T : (p * S // T + 1) * T]
        if at:
            tile = pltpu.roll(tile, T - at, 1)
        isend[p] = tile[:, :S]
    iland[me] = isend[me]
    pl.semaphore_wait(barrier, C + R - 2)

    order = sorted(range(1, C), key=lambda i: -min(i, C - i))
    idx_copies, row_copies = [], []
    for i in order:
        p = to_col(i)
        idx_copies.append(rcopy(isend.at[p], iland.at[me], si.at[i], ri.at[i], {"col": p}))
        idx_copies[-1].start()
    for i in order:
        p = to_col(i)
        row_copies.append(rcopy(uniq.at[p], land.at[me], s1.at[i], r1.at[i], {"col": p}))
        row_copies[-1].start()

    cp_up.start()
    cp_dn.start()

    to, at = iota((256, 256), 0), iota((256, 256), 1)
    perm = (((to & 31) * 8 + (to >> 5)) == at).astype(F32).astype(BF16)
    cp_up.wait()
    for g in range(4):
        blk = matmul(perm, wraw[g * 256 : (g + 1) * 256, :]).astype(BF16)
        for k in range(K):
            wp[k * T + g * 32 : k * T + (g + 1) * 32, :] = blk[k * 32 : (k + 1) * 32, :]
    lane = iota((K, K * T), 1)
    spread = jnp.where((lane & 7) == iota((K, K * T), 0), gain[...], 0.0)
    fold = ((iota((K * T, T), 0) >> 3) == iota((K * T, T), 1)).astype(F32)
    gk = matmul(spread, fold, precision=HIGH)

    amat = jnp.concatenate(
        [
            fmp[...].astype(F32),
            wlc[...].astype(F32),
            wres[...].astype(F32),
        ],
        0,
    )
    for j in range(32):
        arep[j * S : (j + 1) * S, :] = jnp.broadcast_to(amat[j : j + 1, :], (S, T))

    place = (iota((C, T), 0) == (iota((C, T), 1) >> 3)).astype(F32)
    wide = matmul(rid[...].astype(F32).reshape(D * U, C), place, precision=HIGH).reshape(D, U, T)
    mine = iota((D, U, T), 1) == (iota((D, U, T), 2) & (U - 1))
    labels = jnp.sum(jnp.where(mine, wide, 0.0), 1).astype(jnp.int32)
    target = iota((T, T), 0)
    for i in range(R):
        local = labels - to_row(i) * T
        for d in range(D):
            oh[i, d] = jnp.where(
                target == jnp.broadcast_to(local[d : d + 1, :], (T, T)), 1.0, 0.0
            ).astype(BF16)

    for cp in idx_copies:
        cp.wait_recv()
    ix = iland[...].astype(F32).reshape(T, S)
    tiled = (iota((S, T), 0) == (iota((S, T), 1) & (S - 1))).astype(F32)
    idx_n = matmul(ix, tiled, precision=HIGH)
    idxn[...] = idx_n
    idx_t = idx_n.T
    for u in range(U):
        for q in range(4):
            lm[q * T : (q + 1) * T, u * T : (u + 1) * T] = jnp.where(
                idx_t == float(u), arep[q * T : (q + 1) * T, :], 0.0
            ).astype(BF16)
    entry = iota((U, T), 0).astype(F32)

    def fill(src, q):
        for t in range(0, T, 2):
            rows = [
                jnp.where(
                    jnp.broadcast_to(idxn[v : v + 1, :], (U, T)) == entry,
                    jnp.broadcast_to(src[v : v + 1, :], (U, T)),
                    0.0,
                )
                for v in (t, t + 1)
            ]
            lmask[t * U : (t + 2) * U, q * T : (q + 1) * T] = jnp.concatenate(rows, 0).astype(BF16)

    for q in range(4):
        ggr[...] = arep[q * T : (q + 1) * T, :].T
        fill(ggr, q)
    upstream = cot[...].astype(F32)
    for o in range(16):
        rmat[(16 + o) * S : (17 + o) * S, :] = upstream[:, o * E : (o + 1) * E].astype(BF16)

    own_rows.wait()
    for cp in row_copies:
        cp.wait_recv()
    t32[...] = land[...].astype(F32).reshape(T, U * E)
    for u in range(U):
        tst[u * T : (u + 1) * T, :] = t32[:, u * E : (u + 1) * E].astype(BF16)

    comp = matmul(lm[0:T, :], tst[...]).astype(BF16)
    rmat[512:640, :] = comp
    z = matmul(comp, tst[...], NT)
    gram = jnp.where(idx_t == 0.0, z[:, 0:T], 0.0)
    for u in range(1, U):
        gram = gram + jnp.where(idx_t == float(u), z[:, u * T : (u + 1) * T], 0.0)
    n_flat = float(K * T)
    g3 = gram.reshape(K, S, T)
    mu = jnp.sum(jnp.sum(g3, 0), -1, keepdims=True) / n_flat
    cent = g3 - mu[None]
    inv_in = lax.rsqrt(jnp.sum(jnp.sum(cent * cent, 0), -1, keepdims=True) / n_flat + 1e-05)
    normed_in = cent * inv_in[None]
    nrm[...] = normed_in.reshape(K * S, T)
    for k in range(K):
        nall[mr, :, k * T : (k + 1) * T] = (normed_in[k] * gk[k : k + 1, :]).astype(BF16)

    def row_send(stage, src_of, dst):
        copies = []
        for i in range(1, R):
            p = to_row(i)
            sem = stage * R + i
            copies.append(rcopy(src_of(p), dst.at[mr], sx.at[sem], rx.at[sem], {"row": p}))
            copies[-1].start()
        return copies

    n_copies = row_send(0, lambda p: nall.at[mr], nall)
    y[...] = matmul(lm[T:512, :], tst[...])
    cp_dn.wait()
    for cp in n_copies:
        cp.wait_recv()
    hp = matmul(nall[...].reshape(R * S, K * T), wp[...])
    sg = jax.nn.sigmoid(hp)
    hid = (hp * sg).astype(BF16)
    fp = matmul(hid, wd[...]).reshape(R, S, 8 * E)
    fsend[...] = fp.astype(BF16)
    fown[...] = fp
    f_copies = row_send(1, lambda p: fsend.at[p], frecv)
    ds[...] = sg * (1.0 + hp * (1.0 - sg))

    gain_out = og[...]
    up_fm = jnp.concatenate([upstream[:, o * E : (o + 1) * E] for o in range(8)], 0) * gain_out
    up_mean = jnp.mean(up_fm, -1, keepdims=True)

    def out_norm(joined, o):
        up = upstream[:, o * E : (o + 1) * E]
        c = joined - jnp.mean(joined, -1, keepdims=True)
        inv = lax.rsqrt(jnp.mean(c * c, -1, keepdims=True) + 1e-05)
        nr = c * inv
        return nr, norm_back(up * gain_out, nr, inv)

    for o in range(8, 16):
        nr, gj = out_norm(y[(o - 8) * S : (o - 7) * S, :], o)
        lay32[:, o * E : (o + 1) * E] = nr * gain_out + y[(8 + o) * S : (9 + o) * S, :]
        rmat[o * S : (o + 1) * S, :] = gj.astype(BF16)

    for cp in f_copies:
        cp.wait_recv()
    total = fown[mr]
    for i in range(1, R):
        total = total + frecv[from_row(i)].astype(F32)
    fm[...] = total
    joined = jnp.concatenate([fm[:, o * E : (o + 1) * E] for o in range(8)], 0)
    cen = joined - jnp.mean(joined, -1, keepdims=True)
    inv_fm = lax.rsqrt(jnp.mean(cen * cen, -1, keepdims=True) + 1e-05)
    normed_fm = cen * inv_fm
    across = jnp.mean(up_fm * cen, -1, keepdims=True) * inv_fm
    grad_fm = (up_fm - up_mean - normed_fm * across) * inv_fm
    for o in range(8):
        gf32[:, o * E : (o + 1) * E] = grad_fm[o * S : (o + 1) * S]
    gall[mr] = gf32[...].astype(BF16)
    g_copies = row_send(2, lambda p: gall.at[mr], gall)
    for o in range(8):
        lay32[:, o * E : (o + 1) * E] = (
            normed_fm[o * S : (o + 1) * S] * gain_out + y[(8 + o) * S : (9 + o) * S, :]
        )
    lay_out[...] = lay32[...].astype(BF16)
    for cp in g_copies:
        cp.wait_recv()
    gh = matmul(gall[...].reshape(R * S, 8 * E), wd[...], NT)
    gp = (gh * ds[...]).astype(BF16)
    gq = matmul(gp, wp[...], NT).reshape(R, S, K * T)
    qsend[...] = gq.astype(BF16)
    qown[...] = gq
    q_copies = row_send(3, lambda p: qsend.at[p], qrecv)
    for cp in q_copies:
        cp.wait_recv()
    gflat = qown[mr]
    for i in range(1, R):
        gflat = gflat + qrecv[from_row(i)].astype(F32)
    qs = [gflat[:, k * T : (k + 1) * T] * gk[k : k + 1, :] for k in range(K)]
    ns = [nrm[k * S : (k + 1) * S, :] for k in range(K)]
    first = jnp.sum(sum(qs), -1, keepdims=True) / n_flat
    second = jnp.sum(sum(q * n for q, n in zip(qs, ns)), -1, keepdims=True) / n_flat
    for k in range(K):
        ggr[k * S : (k + 1) * S, :] = (qs[k] - first - ns[k] * second) * inv_in
    gg = ggr[...]
    for u in range(U):
        lm[0:T, u * T : (u + 1) * T] = jnp.where(idx_t == float(u), gg, 0.0).astype(BF16)
    ggr[...] = gg.T
    fill(ggr, 4)
    rmat[0:T, :] = matmul(lm[0:T, :], tst[...]).astype(BF16)
    lg[...] = matmul(lmask[...], rmat[...])

    top = lg[:, T:E].reshape(C, D * U, E - T)
    sb[:, 64:96, :] = jnp.concatenate([top[:, :32], top[:, 32:]], -1).astype(BF16)
    sb[:, 0:64, :] = lg[:, 0:T].reshape(C, D * U, T).astype(BF16)
    cuts = (pl.ds(64, 32), pl.ds(0, 32), pl.ds(32, 32))
    sems = ((sbs, rbs), (sa, ra), (sc, rc))
    g_in = []

    def send_lists(stage):
        cut, (ssem, rsem) = cuts[stage], sems[stage]
        g_in.append([])
        for i in order:
            p = to_col(i)
            g_in[stage].append(
                rcopy(sb.at[p, cut], rland.at[me, cut], ssem.at[i], rsem.at[i], {"col": p})
            )
            g_in[stage][-1].start()

    send_lists(0)
    send_lists(1)
    rland[me] = sb[me]

    p_copies = []
    for stage in range(3):
        for cp in g_in[stage]:
            cp.wait_recv()
        pieces = []
        for p in range(2):
            start = (64, 0, 32)[stage] + p * 16
            both = rland[:, start : start + 16, :].astype(F32)
            for h in range(2):
                x = both[:, h * U : (h + 1) * U, :].reshape(T, T).T.astype(BF16)
                d = 2 * p + h
                if stage == 0:
                    pieces.append((d, T, E, x[: E - T]))
                    pieces.append((d + 4, T, E, x[E - T :]))
                else:
                    pieces.append((d + 4 * (stage - 1), 0, T, x))
        for i in range(1, R):
            for d, a, b, x in pieces:
                ps[i, d, a:b, :] = matmul(x, oh[i, d], NT).astype(BF16)
            part = (slice(0, D), slice(T, E)) if stage == 0 else (
                slice(4 * (stage - 1), 4 * stage),
                slice(0, T),
            )
            ds_of = tuple(pl.ds(q.start, q.stop - q.start) for q in part)
            sem = (4 + stage) * R + i
            p_copies.append(
                rcopy(
                    ps.at[(i,) + ds_of],
                    pr.at[(i,) + ds_of],
                    sx.at[sem],
                    rx.at[sem],
                    {"row": to_row(i)},
                )
            )
            p_copies[-1].start()
        if stage == 0:
            send_lists(2)
        for d, a, b, x in pieces:
            rg_out[d, a:b, :] = matmul(x, oh[0, d], NT)
    for cp in p_copies:
        cp.wait_recv()
    for i in range(1, R):
        rg_out[...] += pr[i].astype(F32)

    for group in (
        idx_copies,
        row_copies,
        n_copies,
        f_copies,
        g_copies,
        q_copies,
        g_in[0],
        g_in[1],
        g_in[2],
        p_copies,
    ):
        for cp in group:
            cp.wait_send()


def moment_kernel(width, lay, grads, m1, m2, lay_out, m1_out, m2_out, step_out):
    lay_out[...] = lay[...]
    for h in range(4):
        row = pl.ds(pl.program_id(0) * 4 + h, 1)
        g = grads[h]
        first = 0.9 * m1[h] + 0.1 * g
        second = 0.99 * m2[row, :] + 0.01 * (jnp.sum(g * g, 0, keepdims=True) / width)
        m1_out[h] = first
        m2_out[row, :] = second
        step_out[h] = first * lax.rsqrt(second)


def fast_body(
    C,
    R,
    uniq_rows,
    row_ids,
    sample_idx,
    fm_proj,
    ln_gain,
    w_up,
    w_down,
    w_lc,
    w_res,
    out_gain,
    cotangent,
    moment1,
    moment2,
):
    D = uniq_rows.shape[1]
    S = cotangent.shape[0]
    hid = w_up.shape[1]
    wide = w_down.shape[1]
    flat = w_up.shape[0]
    width = out_gain.shape[0]
    T = C * D
    vmem = pl.BlockSpec(memory_space=pltpu.VMEM)
    hbm = pl.BlockSpec(memory_space=pl.ANY)
    dma = pltpu.SemaphoreType.DMA
    layer_out, row_grads = pl.pallas_call(
        functools.partial(fused_kernel, C, R, D),
        out_shape=(
            jax.ShapeDtypeStruct((S, 16 * width), BF16),
            jax.ShapeDtypeStruct((D, width, T), F32),
        ),
        in_specs=[hbm, vmem, vmem, vmem, vmem, hbm, hbm, vmem, vmem, vmem, vmem],
        out_specs=(vmem, vmem),
        scratch_shapes=[
            pltpu.VMEM((C, D, S), jnp.int32),
            pltpu.VMEM((C, D, wide), BF16),
            pltpu.VMEM((C, D, S), jnp.int32),
            pltpu.VMEM((flat, hid), BF16),
            pltpu.VMEM((flat, hid), BF16),
            pltpu.VMEM((hid, wide), BF16),
            pltpu.VMEM((T, wide), F32),
            pltpu.VMEM((8 * T, width), BF16),
            pltpu.VMEM((512, 8 * T), BF16),
            pltpu.VMEM((8 * T, 640), BF16),
            pltpu.VMEM((512, T), F32),
            pltpu.VMEM((640, width), BF16),
            pltpu.VMEM((128, T), F32),
            pltpu.VMEM((128, T), F32),
            pltpu.VMEM((T, 128), F32),
            pltpu.VMEM((R, S, flat), BF16),
            pltpu.VMEM((384, width), F32),
            pltpu.VMEM((R * S, hid), F32),
            pltpu.VMEM((R, S, wide), F32),
            pltpu.VMEM((R, S, wide), BF16),
            pltpu.VMEM((R, S, wide), BF16),
            pltpu.VMEM((S, wide), F32),
            pltpu.VMEM((R, S, wide), BF16),
            pltpu.VMEM((R, S, flat), F32),
            pltpu.VMEM((R, S, flat), BF16),
            pltpu.VMEM((R, S, flat), BF16),
            pltpu.VMEM((S, 16 * width), F32),
            pltpu.VMEM((S, wide), F32),
            pltpu.VMEM((8 * T, width), F32),
            pltpu.VMEM((C, 12 * D, T), BF16),
            pltpu.VMEM((C, 12 * D, T), BF16),
            pltpu.VMEM((R, D, T, T), BF16),
            pltpu.VMEM((R, D, width, T), BF16),
            pltpu.VMEM((R, D, width, T), BF16),
            dma((4,)),
            dma((C,)),
            dma((C,)),
            dma((C,)),
            dma((C,)),
            dma((C,)),
            dma((C,)),
            dma((C,)),
            dma((C,)),
            dma((C,)),
            dma((C,)),
            dma((7 * R,)),
            dma((7 * R,)),
        ],
        compiler_params=pltpu.CompilerParams(
            collective_id=0, has_side_effects=True, vmem_limit_bytes=56 * 1024 * 1024
        ),
        name="wukong_step",
    )(
        uniq_rows,
        row_ids.transpose(1, 2, 0),
        sample_idx.T,
        fm_proj.T,
        ln_gain.reshape(1, flat),
        w_up,
        w_down,
        w_lc,
        w_res,
        out_gain.reshape(1, width),
        cotangent,
    )
    slab = pl.BlockSpec((4, width, T), lambda d: (d, 0, 0))
    whole = pl.BlockSpec((D, T), lambda d: (0, 0))
    strip = pl.BlockSpec((S, 8 * width), lambda d: (0, d))
    layer_out, new_moment1, new_moment2, row_step = pl.pallas_call(
        functools.partial(moment_kernel, width),
        grid=(D // 4,),
        out_shape=(
            jax.ShapeDtypeStruct((S, 16 * width), BF16),
            jax.ShapeDtypeStruct((D, width, T), F32),
            jax.ShapeDtypeStruct((D, T), F32),
            jax.ShapeDtypeStruct((D, width, T), F32),
        ),
        in_specs=[strip, slab, slab, whole],
        out_specs=(strip, slab, whole, slab),
        name="moments",
    )(layer_out, row_grads, moment1.transpose(0, 2, 1), moment2)
    return (
        layer_out,
        new_moment1.transpose(0, 2, 1),
        new_moment2,
        row_step.transpose(0, 2, 1),
    )


def step(C, R, *args):
    if args[0].shape[1] == 8 and C == 16:
        return fast_body(C, R, *args)
    return plain_body(*args)


def solution(mesh):
    return jax.shard_map(
        functools.partial(step, mesh.shape["col"], mesh.shape["row"]),
        mesh=mesh,
        in_specs=(
            P("row", "col", None),
            P("row", "col", None),
            P("row", "col"),
            P(),
            P(),
            P(None, "row"),
            P("row", None),
            P(),
            P(),
            P(),
            P(("row", "col"), None),
            P("col", "row", None),
            P("col", "row"),
        ),
        out_specs=(
            P(("row", "col"), None),
            P("col", "row", None),
            P("col", "row"),
            P("col", "row", None),
        ),
        check_vma=False,
    )
```
